256 devices in a mesh: alpha: 8 (over z_lo, y), beta: 32 (over z_hi, x, core).
Axes of the slice: x: 4, y: 4, z: 8 (z_hi: 4, z_lo: 2; z = z_hi * 2 + z_lo), core: 2. Of those that a mesh axis runs over, the one named last changes fastest.
Arguments:
- ci_vectors: bfloat16 [8, 4096, 4096], P(None, 'alpha', 'beta'), may hold values from -6 to 6
- alpha_blocks: bfloat16 [32, 16, 128, 128], P('alpha'), may hold values from -0.125 to 0.125
- alpha_cols: int32 [32, 16], P('alpha'), may hold values from 0 to 31, all different within a row
- beta_blocks: bfloat16 [32, 16, 128, 128], P('beta'), may hold values from -0.125 to 0.125
- beta_cols: int32 [32, 16], P('beta'), may hold values from 0 to 31, all different within a row
- diagonal: float32 [4096, 4096], P('alpha', 'beta'), may hold values from -1 to 3
Outputs:
- sigma_vectors: bfloat16 [8, 4096, 4096], P(None, 'alpha', 'beta')
The draws below stay inside these ranges and needn't reach their ends.
Inputs may be any that keep to these rules, and one draw needn't show every extreme that they name: `alpha_cols`: each block-row names 16 different block-columns. `beta_cols`: each block-row names 16 different block-columns.
All inputs are finite; a program needn't handle non-finite values.
Results may differ from the reference program's by a relative error of at most 0.001.
Values may be sent and summed in bfloat16 or wider, within the bound.
A program may use at most 128 MiB of HBM per device.

```python
import jax
import jax.numpy as jnp
from jax import lax

NA = 4096
NB = 4096
BLK = 128
KB = 16
NV = 8
NBLK_A = 32
NBLK_B = 32


def level_of(stream_key, extent, split, smallest, high):
    def one(position, shards_of):
        heights = jax.random.uniform(jax.random.fold_in(jax.random.fold_in(stream_key, 6), position), (shards_of,), jnp.float32, smallest / len(split), high / len(split))
        return jnp.repeat(jnp.exp(heights), extent[position] // shards_of).reshape((-1,) + (1,) * (len(extent) - position - 1))

    factor_of = one(*split[0])
    for cut in split[1:]:
        factor_of = factor_of * one(*cut)
    return factor_of


def choose_distinct(key, rows, count, top, lift):
    sequence = jax.random.permutation(jax.random.fold_in(key, 1), count)
    pull = sequence
    for power in range(3):
        pull = pull * pull // count
    pull = pull * lift // count
    tickets = jax.random.randint(jax.random.fold_in(key, 2), (rows, count), 0, 4096) + pull
    holders = jax.random.permutation(jax.random.fold_in(key, 3), rows)[jnp.arange(count) % rows]
    tickets = jnp.where(jnp.arange(rows)[:, None] == holders[None, :], 1 << 14, tickets)
    score = tickets * count + jnp.arange(count)
    return lax.top_k(score.astype(jnp.int32), top)[1].astype(jnp.int32)


def scatter_about(stream_key, extent, width, most, split=(), kind=jnp.bfloat16):
    entries = jax.random.normal(stream_key, extent, jnp.float32) * width
    if len(split) > 0:
        entries = level_of(stream_key, extent, split, -0.22, 0.18) * entries
    return jnp.clip(entries, min=-most, max=most).astype(kind)


def setup_inputs(seed: int = 0) -> dict:
    seeds = jax.random.split(jax.random.key(seed), 7)
    ci_vectors = scatter_about(seeds[0], (NV, NA, NB), 1.0, 6.0, ((1, 8), (2, 32)))
    alpha_blocks = scatter_about(seeds[1], (NBLK_A, KB, BLK, BLK), (KB * BLK) ** -0.5, 0.125, ((0, 8),))
    alpha_cols = choose_distinct(seeds[2], NBLK_A, NBLK_A, KB, 0)
    beta_blocks = scatter_about(seeds[3], (NBLK_B, KB, BLK, BLK), (KB * BLK) ** -0.5, 0.125, ((0, 32),))
    beta_cols = choose_distinct(seeds[4], NBLK_B, NBLK_B, KB, 0)
    diagonal = jnp.clip(-1.0 + 4.0 * jax.random.uniform(seeds[5], (NA, NB), jnp.float32) ** level_of(seeds[5], (NA, NB), ((0, 8), (1, 32)), -0.2, 0.2), -1.0, 3.0)
    return {"ci_vectors": ci_vectors, "alpha_blocks": alpha_blocks, "alpha_cols": alpha_cols, "beta_blocks": beta_blocks, "beta_cols": beta_cols, "diagonal": diagonal}


def alpha_term(ci_vectors, alpha_blocks, alpha_cols):
    grid = ci_vectors.reshape(NV, NBLK_A, BLK, NB)

    def one_row(pair):
        blocks, columns = pair
        picked = grid[:, columns].astype(jnp.float32)
        return jnp.einsum('kij,vkjb->vib', blocks.astype(jnp.float32), picked)

    stacked = lax.map(one_row, (alpha_blocks, alpha_cols))
    return stacked.transpose(1, 0, 2, 3).reshape(NV, NA, NB)


def beta_term(ci_vectors, beta_blocks, beta_cols):
    grid = ci_vectors.reshape(NV, NA, NBLK_B, BLK)

    def one_row(pair):
        blocks, columns = pair
        picked = grid[:, :, columns].astype(jnp.float32)
        return jnp.einsum('vakj,kij->vai', picked, blocks.astype(jnp.float32))

    stacked = lax.map(one_row, (beta_blocks, beta_cols))
    return stacked.transpose(1, 2, 0, 3).reshape(NV, NA, NB)


def reference(ci_vectors, alpha_blocks, alpha_cols, beta_blocks, beta_cols, diagonal):
    alpha_part = alpha_term(ci_vectors, alpha_blocks, alpha_cols)
    beta_part = beta_term(ci_vectors, beta_blocks, beta_cols)
    total = alpha_part + beta_part + diagonal[None, :, :] * ci_vectors.astype(jnp.float32)
    return total.astype(jnp.bfloat16)
```

```python
import functools

import jax
import jax.numpy as jnp
from jax import lax
from jax.experimental import pallas as pl
from jax.experimental.pallas import tpu as pltpu
from jax.sharding import PartitionSpec as P

MESH = pl.DeviceIdType.MESH
BF = jnp.bfloat16
F32 = jnp.float32


def kernel(
    c_ref, a_ref, b_ref, ta_ref, tb_ref, d_ref, out_ref,
    ca, cs, co, abuf, bbuf, ia, ib, sa, sb, dg, ad, bd, acc, sig,
    ss, rs, ls,
):
    i = lax.axis_index("alpha")
    j = lax.axis_index("beta")
    l = i // 4
    y = i % 4
    c = j % 2
    x = (j // 2) % 4
    h = j // 8
    z = 2 * h + l

    def dev(xx, yy, zz, cc):
        return ((zz % 2) * 4 + yy, ((zz // 2) * 4 + xx) * 2 + cc)

    def zdev(zz):
        return dev(x, y, zz, c)

    zr = (z + 1) % 8
    zl = (z + 7) % 8
    zin = 2 * h + (1 - l)
    zout = (z + 7 + 2 * l) % 8
    d_xr = dev((x + 1) % 4, y, z, c)
    d_xl = dev((x + 3) % 4, y, z, c)
    d_yr = dev(x, (y + 1) % 4, z, c)
    d_yl = dev(x, (y + 3) % 4, z, c)
    d_co = dev(x, y, z, 1 - c)

    barrier = pltpu.get_barrier_semaphore()
    peers = [zdev((z + d) % 8) for d in range(1, 8)] + [d_xr, d_xl, d_yr, d_yl, d_co]
    for p in peers:
        pl.semaphore_signal(barrier, inc=1, device_id=p, device_id_type=MESH)
    pl.semaphore_wait(barrier, len(peers))

    count = [0]
    sent = []

    def put(src, dst, device):
        k = count[0]
        count[0] += 1
        copy = pltpu.make_async_remote_copy(
            src_ref=src, dst_ref=dst, send_sem=ss.at[k], recv_sem=rs.at[k],
            device_id=device, device_id_type=MESH,
        )
        copy.start()
        sent.append(copy)
        return copy

    lcount = [0]

    def move(src, dst):
        k = lcount[0]
        lcount[0] += 1
        copy = pltpu.make_async_copy(src, dst, ls.at[k])
        copy.start()
        return copy

    own_c = move(c_ref.at[z], ca.at[0, z])
    c_in = []
    for d in (4, 3, 5, 2, 6, 1, 7):
        zz = (z + d) % 8
        c_in.append(put(c_ref.at[zz], ca.at[0, z], zdev(zz)))
    b1 = put(b_ref.at[0], bbuf.at[1, pl.ds(0, 16)], zdev(zout))
    tb1 = put(tb_ref, ib.at[1], zdev(zout))
    a_in = [
        put(a_ref.at[2 * c], abuf.at[4 * l + 2 * c, pl.ds(0, 16)], zdev(zin)),
        put(a_ref.at[2 * c + 1], abuf.at[4 * l + 2 * c + 1, pl.ds(0, 16)], zdev(jnp.where(c == 0, zin, zout))),
    ]
    ta1 = put(ta_ref, ia.at[l], zdev(zin))
    dr = put(d_ref, dg.at[z], zdev(zr))
    dl = put(d_ref, dg.at[z], zdev(zl))
    own = [
        move(a_ref.at[r], abuf.at[4 * l + r, pl.ds(0, 16)]) for r in range(4)
    ] + [
        move(b_ref.at[0], bbuf.at[0, pl.ds(0, 16)]),
        move(ta_ref, ia.at[l]),
        move(tb_ref, ib.at[0]),
        move(d_ref, dg.at[z]),
    ]
    zero = jnp.zeros((128, 128), BF)
    for r in range(8):
        abuf[r, 16] = zero
    for r in range(4):
        bbuf[r, 16] = zero

    own_c.wait()
    for copy in c_in:
        copy.wait_recv()
    mine = ca.at[0]
    yr = put(mine, ca.at[1], d_yr)
    yl = put(mine, ca.at[2], d_yl)
    xr = put(mine, cs.at[0], d_xr)
    xl = put(mine, cs.at[1], d_xl)
    o0 = put(mine, co.at[0], d_co)

    b1.wait_recv()
    b2 = put(bbuf.at[1, pl.ds(0, 16)], bbuf.at[2, pl.ds(0, 16)], zdev(zin))
    tb1.wait_recv()
    tb2 = put(ib.at[1], ib.at[2], zdev(zin))

    def dstep(s, half):
        right = (z + 8 - s) % 8
        left = (z + s) % 8
        if half:
            lo, hi = pl.ds(0, 256), pl.ds(256, 256)
            return (
                put(dg.at[right, lo], dg.at[right, lo], zdev(zr)),
                put(dg.at[left, hi], dg.at[left, hi], zdev(zl)),
            )
        return (
            put(dg.at[right], dg.at[right], zdev(zr)),
            put(dg.at[left], dg.at[left], zdev(zl)),
        )

    dr.wait_recv()
    dl.wait_recv()
    dr, dl = dstep(1, False)
    for copy in a_in:
        copy.wait_recv()
    other = 4 * (1 - l)
    a_x = [
        put(abuf.at[other + 2 * c + k, pl.ds(0, 16)], abuf.at[other + 2 * c + k, pl.ds(0, 16)], d_co)
        for k in range(2)
    ]

    lo, hi = pl.ds(0, 4), pl.ds(4, 4)
    xr.wait_recv()
    xr2 = put(cs.at[0, lo], cs.at[2, lo], d_xr)
    o1 = put(cs.at[0], co.at[1], d_co)
    xl.wait_recv()
    xl2 = put(cs.at[1, hi], cs.at[2, hi], d_xl)
    o2 = put(cs.at[1], co.at[2], d_co)
    yr.wait_recv()
    yr2 = put(ca.at[1, lo], ca.at[3, lo], d_yr)
    yl.wait_recv()
    yl2 = put(ca.at[2, hi], ca.at[3, hi], d_yl)

    b2.wait_recv()
    b3 = put(bbuf.at[2, pl.ds(0, 16)], bbuf.at[3, pl.ds(0, 16)], zdev(zout))
    tb2.wait_recv()
    tb3 = put(ib.at[2], ib.at[3], zdev(zout))
    dr.wait_recv()
    dl.wait_recv()
    dr, dl = dstep(2, False)

    for copy in own:
        copy.wait()
    ta1.wait_recv()
    for copy in a_x:
        copy.wait_recv()
    ta_s = [move(ia, sa)]
    for copy in ta_s:
        copy.wait()

    ys = [y, (y + 3) % 4, (y + 1) % 4, (y + 2) % 4]

    def fill_a(s):
        def body(k, carry):
            col = ((k // 4) * 4 + ys[s]) * 4 + k % 4
            for r in range(8):
                at = sa[r // 4, r % 4, col]
                ad[s, pl.ds(r * 128, 128), pl.ds(pl.multiple_of(k * 128, 128), 128)] = abuf[r, at]
            return carry

        lax.fori_loop(0, 8, body, 0)

    for s in range(4):
        fill_a(s)

    def alpha_dot(s, first):
        def body(m, carry):
            wide = jnp.concatenate(
                [ca[s, pl.ds(2 * q, 2)].reshape(1024, 128) for q in range(4)], axis=1
            )
            lhs = ad[s, pl.ds(pl.multiple_of(m * 256, 256), 256), :]
            res = jnp.dot(lhs, wide, preferred_element_type=F32)
            low = m // 2
            rows = pl.ds(pl.multiple_of((m % 2) * 256, 256), 256)
            for q in range(4):
                piece = res[:, q * 128:(q + 1) * 128]
                if first:
                    acc[2 * q + low, rows, :] = piece
                else:
                    acc[2 * q + low, rows, :] += piece
            return carry

        lax.fori_loop(0, 4, body, 0)

    alpha_dot(0, True)
    alpha_dot(1, False)
    alpha_dot(2, False)

    b3.wait_recv()
    tb3.wait_recv()
    tb_s = move(ib, sb)
    tb_s.wait()
    dr.wait_recv()
    dl.wait_recv()
    dr, dl = dstep(3, True)

    near = (h + 3 + 2 * l) % 4
    far = (h + 1 + 2 * l) % 4
    hs = [h, near, far, (h + 2) % 4]
    xs = [x, (x + 3) % 4, (x + 1) % 4, (x + 2) % 4]

    def fill_b(s):
        cc = c if s < 4 else 1 - c
        xx = xs[s % 4]

        def body(k, carry):
            col = (k * 4 + xx) * 2 + cc
            for r in range(4):
                at = sb[r, 0, col]
                rows = pl.ds(pl.multiple_of(hs[r] * 128, 128), 128)
                bd[s, rows, pl.ds(pl.multiple_of(k * 128, 128), 128)] = bbuf[r, at]
            return carry

        lax.fori_loop(0, 4, body, 0)

    for s in range(8):
        fill_b(s)

    def beta_dot(s):
        if s == 0:
            src = ca.at[0]
        elif s < 4:
            src = cs.at[s - 1]
        else:
            src = co.at[s - 4]

        def body(m, carry):
            low = m // 2
            rows = pl.ds(pl.multiple_of((m % 2) * 256, 256), 256)
            lhs = jnp.concatenate([src[2 * q + low, rows, :] for q in range(4)], axis=1)
            res = lax.dot_general(lhs, bd[s], (((1,), (1,)), ((), ())), preferred_element_type=F32)
            for q in range(4):
                acc[2 * q + low, rows, :] += res[:, q * 128:(q + 1) * 128]
            return carry

        lax.fori_loop(0, 4, body, 0)

    beta_dot(0)
    beta_dot(1)
    beta_dot(2)
    o0.wait_recv()
    beta_dot(4)
    o1.wait_recv()
    beta_dot(5)
    o2.wait_recv()
    beta_dot(6)
    xr2.wait_recv()
    xl2.wait_recv()
    o3 = put(cs.at[2], co.at[3], d_co)
    beta_dot(3)
    yr2.wait_recv()
    yl2.wait_recv()
    alpha_dot(3, False)
    o3.wait_recv()
    beta_dot(7)
    dr.wait_recv()
    dl.wait_recv()

    outs = []
    for d in (4, 3, 5, 2, 6, 1, 7, 0):
        zz = (z + d) % 8
        sig[zz] = (acc[zz] + dg[zz] * ca[0, zz].astype(F32)).astype(BF)
        if d:
            outs.append(put(sig.at[zz], out_ref.at[z], zdev(zz)))
        else:
            last = move(sig.at[zz], out_ref.at[zz])
    last.wait()
    for copy in outs:
        copy.wait_recv()
    for copy in sent:
        copy.wait_send()


def slots(cols):
    hit = cols[:, None, :] == jnp.arange(32, dtype=jnp.int32)[None, :, None]
    order = jnp.arange(16, dtype=jnp.int32)
    table = jnp.min(jnp.where(hit, order, 16), axis=-1).astype(jnp.int32)
    return jnp.pad(table, ((0, 8 - table.shape[0]), (0, 96)))


def shards(ci_vectors, alpha_blocks, alpha_cols, beta_blocks, beta_cols, diagonal):
    anywhere = pl.BlockSpec(memory_space=pl.ANY)
    hbm = pl.BlockSpec(memory_space=pltpu.MemorySpace.HBM)
    return pl.pallas_call(
        kernel,
        out_shape=jax.ShapeDtypeStruct((8, 512, 128), BF),
        in_specs=[hbm] * 6,
        out_specs=hbm,
        scratch_shapes=[
            pltpu.VMEM((4, 8, 512, 128), BF),
            pltpu.VMEM((3, 8, 512, 128), BF),
            pltpu.VMEM((4, 8, 512, 128), BF),
            pltpu.VMEM((8, 17, 128, 128), BF),
            pltpu.VMEM((4, 17, 128, 128), BF),
            pltpu.VMEM((2, 8, 128), jnp.int32),
            pltpu.VMEM((4, 8, 128), jnp.int32),
            pltpu.SMEM((2, 8, 128), jnp.int32),
            pltpu.SMEM((4, 8, 128), jnp.int32),
            pltpu.VMEM((8, 512, 128), F32),
            pltpu.VMEM((4, 1024, 1024), BF),
            pltpu.VMEM((8, 512, 512), BF),
            pltpu.VMEM((8, 512, 128), F32),
            pltpu.VMEM((8, 512, 128), BF),
            pltpu.SemaphoreType.DMA((64,)),
            pltpu.SemaphoreType.DMA((64,)),
            pltpu.SemaphoreType.DMA((16,)),
        ],
        compiler_params=pltpu.CompilerParams(
            collective_id=0, has_side_effects=True, vmem_limit_bytes=60 * 1024 * 1024
        ),
    )(ci_vectors, alpha_blocks, beta_blocks, slots(alpha_cols), slots(beta_cols), diagonal)


def solution(mesh):
    placed = (
        P(None, "alpha", "beta"),
        P("alpha", None, None, None),
        P("alpha", None),
        P("beta", None, None, None),
        P("beta", None),
        P("alpha", "beta"),
    )
    return jax.shard_map(
        shards, mesh=mesh, in_specs=placed, out_specs=P(None, "alpha", "beta"), check_vma=False
    )
```

```python
import jax
import jax.numpy as jnp
from jax import lax
from jax.experimental import pallas as pl
from jax.experimental.pallas import tpu as pltpu
from jax.sharding import PartitionSpec as P

MESH = pl.DeviceIdType.MESH
BF = jnp.bfloat16
F32 = jnp.float32


def kernel(
    c_ref, a_ref, b_ref, t_ref, d_ref, out_ref,
    ca, cs, co, abuf, bbuf, ia, ib, sa, sb, dg, ad, bd, acc, sig,
    ss, rs, ls,
):
    i = lax.axis_index("alpha")
    j = lax.axis_index("beta")
    l = i // 4
    y = i % 4
    c = j % 2
    x = (j // 2) % 4
    h = j // 8
    z = 2 * h + l

    def dev(xx, yy, zz, cc):
        return ((zz % 2) * 4 + yy, ((zz // 2) * 4 + xx) * 2 + cc)

    def zdev(zz):
        return dev(x, y, zz, c)

    zr = (z + 1) % 8
    zl = (z + 7) % 8
    zin = 2 * h + (1 - l)
    zout = (z + 7 + 2 * l) % 8
    d_xr = dev((x + 1) % 4, y, z, c)
    d_xl = dev((x + 3) % 4, y, z, c)
    d_yr = dev(x, (y + 1) % 4, z, c)
    d_yl = dev(x, (y + 3) % 4, z, c)
    d_co = dev(x, y, z, 1 - c)

    barrier = pltpu.get_barrier_semaphore()
    peers = [zdev((z + d) % 8) for d in range(1, 8)] + [d_xr, d_xl, d_yr, d_yl, d_co]
    for p in peers:
        pl.semaphore_signal(barrier, inc=1, device_id=p, device_id_type=MESH)
    pl.semaphore_wait(barrier, len(peers))

    count = [0]
    sent = []

    def put(src, dst, device):
        k = count[0]
        count[0] += 1
        copy = pltpu.make_async_remote_copy(
            src_ref=src, dst_ref=dst, send_sem=ss.at[k], recv_sem=rs.at[k],
            device_id=device, device_id_type=MESH,
        )
        copy.start()
        sent.append(copy)
        return copy

    lcount = [0]

    def move(src, dst):
        k = lcount[0]
        lcount[0] += 1
        copy = pltpu.make_async_copy(src, dst, ls.at[k])
        copy.start()
        return copy

    cuts = ((0, 128), (128, 128), (256, 256))
    chunk = [pl.ds(a, n) for a, n in cuts]
    own_c = move(c_ref.at[z], ca.at[0, z])
    c_in = ([], [], [])

    def turn(k):
        for d in (4, 3, 5, 2, 6, 1, 7):
            zz = (z + d) % 8
            c_in[k].append(put(c_ref.at[zz, chunk[k]], ca.at[0, z, chunk[k]], zdev(zz)))

    quarter = pl.ds(4 * y, 4)
    part = pl.ds(8 * c, 8)
    b1 = put(b_ref.at[0, quarter], bbuf.at[1, quarter], zdev(zout))
    tb_in = [put(t_ref, ib.at[d], zdev((z + 8 + (2 * l - 1) * d) % 8)) for d in (3, 2, 1)]
    ta_in = put(t_ref, ia.at[l], zdev(zin))
    turn(0)
    a_in = put(a_ref.at[x, part], abuf.at[4 * l + x, part], zdev(jnp.where(c == 0, zin, zout)))
    own = [
        move(a_ref.at[r], abuf.at[4 * l + r, pl.ds(0, 16)]) for r in range(4)
    ] + [
        move(b_ref.at[0], bbuf.at[0, pl.ds(0, 16)]),
        move(t_ref, ia.at[l]),
        move(t_ref, ib.at[0]),
        move(d_ref, dg.at[z]),
    ]
    zero = jnp.zeros((128, 128), BF)
    for r in range(8):
        abuf[r, 16] = zero
    for r in range(4):
        bbuf[r, 16] = zero

    full, lo, hi = pl.ds(0, 8), pl.ds(0, 4), pl.ds(4, 4)

    def spread(k):
        for copy in c_in[k]:
            copy.wait_recv()
        mine = ca.at[0, full, chunk[k]]
        return (
            put(mine, ca.at[1, full, chunk[k]], d_yr),
            put(mine, cs.at[0, full, chunk[k]], d_xr),
            put(mine, ca.at[2, full, chunk[k]], d_yl),
            put(mine, cs.at[1, full, chunk[k]], d_xl),
            put(mine, co.at[0, full, chunk[k]], d_co),
        )

    def across_x(k, first):
        _, xr, _, xl, _ = first
        xr.wait_recv()
        xr2 = put(cs.at[0, lo, chunk[k]], cs.at[2, lo, chunk[k]], d_xr)
        xl.wait_recv()
        xl2 = put(cs.at[1, hi, chunk[k]], cs.at[2, hi, chunk[k]], d_xl)
        o = put(cs.at[pl.ds(0, 2), full, chunk[k]], co.at[pl.ds(1, 2), full, chunk[k]], d_co)
        return xr2, xl2, o

    def across_y(k, first):
        yr, _, yl, _, _ = first
        yr.wait_recv()
        yr2 = put(ca.at[1, lo, chunk[k]], ca.at[3, lo, chunk[k]], d_yr)
        yl.wait_recv()
        yl2 = put(ca.at[2, hi, chunk[k]], ca.at[3, hi, chunk[k]], d_yl)
        return yr2, yl2

    def last_core(k, second):
        second[0].wait_recv()
        second[1].wait_recv()
        return put(cs.at[2, full, chunk[k]], co.at[3, full, chunk[k]], d_co)

    def dstep(s, half):
        right = (z + 8 - s) % 8
        left = (z + s) % 8
        if half:
            rlo, rhi = pl.ds(0, 256), pl.ds(256, 256)
            return (
                put(dg.at[right, rlo], dg.at[right, rlo], zdev(zr)),
                put(dg.at[left, rhi], dg.at[left, rhi], zdev(zl)),
            )
        return (
            put(dg.at[right], dg.at[right], zdev(zr)),
            put(dg.at[left], dg.at[left], zdev(zl)),
        )

    b1.wait_recv()
    b2 = put(bbuf.at[1, quarter], bbuf.at[2, quarter], zdev(zin))
    turn(1)
    own_c.wait()
    f0 = spread(0)
    b2.wait_recv()
    b3 = put(bbuf.at[2, quarter], bbuf.at[3, quarter], zdev(zout))
    turn(2)
    dr = put(d_ref, dg.at[z], zdev(zr))
    dl = put(d_ref, dg.at[z], zdev(zl))
    other = 4 * (1 - l)
    a_in.wait_recv()
    piece = abuf.at[other + x, part]
    axr = put(piece, piece, d_xr)
    axl = put(piece, piece, d_xl)
    n0 = across_x(0, f0)
    m0 = across_y(0, f0)
    f1 = spread(1)
    b3.wait_recv()
    three = pl.ds(1, 3)
    piece = bbuf.at[three, quarter]
    byr = put(piece, piece, d_yr)
    byl = put(piece, piece, d_yl)
    axr.wait_recv()
    piece = abuf.at[other + (x + 3) % 4, pl.ds(8 * c, 4)]
    axr2 = put(piece, piece, d_xr)
    axl.wait_recv()
    piece = abuf.at[other + (x + 1) % 4, pl.ds(8 * c + 4, 4)]
    axl2 = put(piece, piece, d_xl)
    o0 = last_core(0, n0)
    n1 = across_x(1, f1)
    m1 = across_y(1, f1)
    axr2.wait_recv()
    axl2.wait_recv()
    piece = abuf.at[pl.ds(other, 4), part]
    a_x = put(piece, piece, d_co)

    for copy in own:
        copy.wait()
    ta_in.wait_recv()
    for copy in tb_in:
        copy.wait_recv()
    ta_s = move(ia, sa)
    tb_s = move(ib, sb)
    ta_s.wait()
    tb_s.wait()
    o1 = last_core(1, n1)
    a_x.wait_recv()
    ys = [y, (y + 3) % 4, (y + 1) % 4, (y + 2) % 4]

    def fill_a(s):
        def body(t, carry):
            col = ((t // 2 % 2) * 4 + ys[s]) * 4 + (t // 4) * 2 + t % 2
            for r in range(8):
                at = sa[r // 4, r % 4, col]
                ad[s, pl.ds(r * 128, 128), pl.ds(pl.multiple_of(t * 128, 128), 128)] = abuf[r, at]
            return carry

        lax.fori_loop(0, 8, body, 0)

    for s in range(4):
        fill_a(s)

    half = (pl.ds(0, 256), pl.ds(256, 256))

    def alpha_dot(s, k, fresh=False):
        wide = jnp.concatenate(
            [ca[s, pl.ds(2 * q, 2), half[k]].reshape(512, 128) for q in range(4)], axis=1
        )
        res = jnp.dot(ad[s, :, pl.ds(512 * k, 512)], wide, preferred_element_type=F32)
        for q in range(4):
            piece = res[:, q * 128:(q + 1) * 128].reshape(2, 512, 128)
            if fresh:
                acc[pl.ds(2 * q, 2)] = piece
            else:
                acc[pl.ds(2 * q, 2)] += piece

    near = (h + 3 + 2 * l) % 4
    far = (h + 1 + 2 * l) % 4
    hs = [h, near, far, (h + 2) % 4]
    xs = [x, (x + 3) % 4, (x + 1) % 4, (x + 2) % 4]

    def fill_b(s):
        cc = c if s < 4 else 1 - c
        xx = xs[s % 4]

        def body(t, carry):
            col = (t * 4 + xx) * 2 + cc
            for r in range(4):
                at = sb[r, 4, col]
                rows = pl.ds(pl.multiple_of(hs[r] * 128, 128), 128)
                bd[s, rows, pl.ds(pl.multiple_of(t * 128, 128), 128)] = bbuf[r, at]
            return carry

        lax.fori_loop(0, 4, body, 0)

    def beta_dot(s, k):
        if s == 0:
            src = ca.at[0]
        elif s < 4:
            src = cs.at[s - 1]
        else:
            src = co.at[s - 4]

        lhs = jnp.concatenate(
            [src[pl.ds(2 * q, 2), half[k], :].reshape(512, 128) for q in range(4)], axis=1
        )
        res = lax.dot_general(lhs, bd[s], (((1,), (1,)), ((), ())), preferred_element_type=F32)
        for q in range(4):
            acc[pl.ds(2 * q, 2), half[k], :] += res[:, q * 128:(q + 1) * 128].reshape(2, 256, 128)

    byr.wait_recv()
    piece = bbuf.at[three, pl.ds(4 * ((y + 3) % 4), 2)]
    byr2 = put(piece, piece, d_yr)
    byl.wait_recv()
    piece = bbuf.at[three, pl.ds(4 * ((y + 1) % 4) + 2, 2)]
    byl2 = put(piece, piece, d_yl)
    f2 = spread(2)
    alpha_dot(0, 0, True)
    alpha_dot(1, 0)
    alpha_dot(2, 0)
    for copy in m0 + m1:
        copy.wait_recv()
    alpha_dot(3, 0)
    dr.wait_recv()
    dl.wait_recv()
    dr, dl = dstep(1, False)
    byr2.wait_recv()
    byl2.wait_recv()
    for s in range(8):
        fill_b(s)
    for s in range(4):
        beta_dot(s, 0)
    f0[4].wait_recv()
    f1[4].wait_recv()
    dr.wait_recv()
    dl.wait_recv()
    dr, dl = dstep(2, False)
    beta_dot(4, 0)
    n0[2].wait_recv()
    n1[2].wait_recv()
    beta_dot(5, 0)
    beta_dot(6, 0)
    n2 = across_x(2, f2)
    o0.wait_recv()
    o1.wait_recv()
    beta_dot(7, 0)
    alpha_dot(0, 1)
    beta_dot(0, 1)
    dr.wait_recv()
    dl.wait_recv()
    dr, dl = dstep(3, True)
    m2 = across_y(2, f2)
    beta_dot(1, 1)
    beta_dot(2, 1)
    o2 = last_core(2, n2)
    f2[4].wait_recv()
    beta_dot(4, 1)
    n2[2].wait_recv()
    beta_dot(5, 1)
    beta_dot(6, 1)
    beta_dot(3, 1)
    alpha_dot(1, 1)
    alpha_dot(2, 1)
    o2.wait_recv()
    beta_dot(7, 1)
    for copy in m2:
        copy.wait_recv()
    alpha_dot(3, 1)
    dr.wait_recv()
    dl.wait_recv()

    outs = []
    for d in (4, 3, 5, 2, 6, 1, 7, 0):
        zz = (z + d) % 8

        def finish(t, carry):
            rows = pl.ds(pl.multiple_of(t * 128, 128), 128)
            whole = acc[zz, rows] + dg[zz, rows] * ca[0, zz, rows].astype(F32)
            sig[zz, rows] = whole.astype(BF)
            return carry

        lax.fori_loop(0, 4, finish, 0)
        if d:
            outs.append(put(sig.at[zz], out_ref.at[z], zdev(zz)))
        else:
            last = move(sig.at[zz], out_ref.at[zz])
    last.wait()
    for copy in outs:
        copy.wait_recv()
    for copy in sent:
        copy.wait_send()


def slots(alpha_cols, beta_cols):
    rows = jnp.arange(8)[:, None, None]
    a = jnp.pad(alpha_cols, ((0, 4), (0, 0)))[:, None, :]
    cols = jnp.where(rows == 4, beta_cols[None], a)
    hit = cols == jnp.arange(128, dtype=jnp.int32)[None, :, None]
    return jnp.min(jnp.where(hit, jnp.arange(16, dtype=jnp.int32), 16), axis=-1)


def shards(ci_vectors, alpha_blocks, alpha_cols, beta_blocks, beta_cols, diagonal):
    hbm = pl.BlockSpec(memory_space=pltpu.MemorySpace.HBM)
    return pl.pallas_call(
        kernel,
        out_shape=jax.ShapeDtypeStruct((8, 512, 128), BF),
        in_specs=[hbm] * 5,
        out_specs=hbm,
        scratch_shapes=[
            pltpu.VMEM((4, 8, 512, 128), BF),
            pltpu.VMEM((3, 8, 512, 128), BF),
            pltpu.VMEM((4, 8, 512, 128), BF),
            pltpu.VMEM((8, 17, 128, 128), BF),
            pltpu.VMEM((4, 17, 128, 128), BF),
            pltpu.VMEM((2, 8, 128), jnp.int32),
            pltpu.VMEM((4, 8, 128), jnp.int32),
            pltpu.SMEM((2, 8, 128), jnp.int32),
            pltpu.SMEM((4, 8, 128), jnp.int32),
            pltpu.VMEM((8, 512, 128), F32),
            pltpu.VMEM((4, 1024, 1024), BF),
            pltpu.VMEM((8, 512, 512), BF),
            pltpu.VMEM((8, 512, 128), F32),
            pltpu.VMEM((8, 512, 128), BF),
            pltpu.SemaphoreType.DMA((112,)),
            pltpu.SemaphoreType.DMA((112,)),
            pltpu.SemaphoreType.DMA((16,)),
        ],
        compiler_params=pltpu.CompilerParams(
            collective_id=0, has_side_effects=True, vmem_limit_bytes=60 * 1024 * 1024
        ),
    )(ci_vectors, alpha_blocks, beta_blocks, slots(alpha_cols, beta_cols), diagonal)


def solution(mesh):
    placed = (
        P(None, "alpha", "beta"),
        P("alpha", None, None, None),
        P("alpha", None),
        P("beta", None, None, None),
        P("beta", None),
        P("alpha", "beta"),
    )
    return jax.shard_map(
        shards, mesh=mesh, in_specs=placed, out_specs=P(None, "alpha", "beta"), check_vma=False
    )
```

```python
import jax
import jax.numpy as jnp
from jax import lax
from jax.experimental import pallas as pl
from jax.experimental.pallas import tpu as pltpu
from jax.sharding import PartitionSpec as P

MESH = pl.DeviceIdType.MESH
BF = jnp.bfloat16
F32 = jnp.float32


def kernel(
    c_ref, a_ref, ac_ref, b_ref, bc_ref, d_ref, out_ref,
    ca, cs, co, abuf, bbuf, tab, ia, ib, sac, sbc, sa, sb, dg, ad, bd, acc, sig,
    ss, rs, ls,
):
    i = lax.axis_index("alpha")
    j = lax.axis_index("beta")
    l = i // 4
    y = i % 4
    c = j % 2
    x = (j // 2) % 4
    h = j // 8
    z = 2 * h + l

    def dev(xx, yy, zz, cc):
        return ((zz % 2) * 4 + yy, ((zz // 2) * 4 + xx) * 2 + cc)

    def zdev(zz):
        return dev(x, y, zz, c)

    zr = (z + 1) % 8
    zl = (z + 7) % 8
    zin = 2 * h + (1 - l)
    zout = (z + 7 + 2 * l) % 8
    d_xr = dev((x + 1) % 4, y, z, c)
    d_xl = dev((x + 3) % 4, y, z, c)
    d_yr = dev(x, (y + 1) % 4, z, c)
    d_yl = dev(x, (y + 3) % 4, z, c)
    d_co = dev(x, y, z, 1 - c)

    barrier = pltpu.get_barrier_semaphore()
    peers = [zdev((z + d) % 8) for d in range(1, 8)] + [d_xr, d_xl, d_yr, d_yl, d_co]
    for p in peers:
        pl.semaphore_signal(barrier, inc=1, device_id=p, device_id_type=MESH)
    pl.semaphore_wait(barrier, len(peers))

    count = [0]
    sent = []

    def put(src, dst, device):
        k = count[0]
        count[0] += 1
        copy = pltpu.make_async_remote_copy(
            src_ref=src, dst_ref=dst, send_sem=ss.at[k], recv_sem=rs.at[k],
            device_id=device, device_id_type=MESH,
        )
        copy.start()
        sent.append(copy)
        return copy

    lcount = [0]

    def move(src, dst):
        k = lcount[0]
        lcount[0] += 1
        copy = pltpu.make_async_copy(src, dst, ls.at[k])
        copy.start()
        return copy

    cols_in = [move(ac_ref, sac), move(bc_ref, sbc)]
    chunk = [pl.ds(128 * k, 128) for k in range(4)]
    half = (pl.ds(0, 256), pl.ds(256, 256))
    own_c = move(c_ref.at[z], ca.at[0, z])
    c_in = ([], [], [], [])

    def turn(k):
        for d in (4, 3, 5, 2, 6, 1, 7):
            zz = (z + d) % 8
            c_in[k].append(put(c_ref.at[zz, chunk[k]], ca.at[0, z, chunk[k]], zdev(zz)))

    quarter = pl.ds(4 * y, 4)
    part = pl.ds(8 * c, 8)
    turn(0)
    b1 = put(b_ref.at[0, quarter], bbuf.at[1, quarter], zdev(zout))
    turn(1)
    a_in = put(a_ref.at[x, part], abuf.at[4 * l + x, part], zdev(jnp.where(c == 0, zin, zout)))
    own = [
        move(a_ref.at[r], abuf.at[4 * l + r, pl.ds(0, 16)]) for r in range(4)
    ] + [
        move(b_ref.at[0], bbuf.at[0, pl.ds(0, 16)]),
        move(d_ref, dg.at[z]),
    ]
    zero = jnp.zeros((128, 128), BF)
    for r in range(8):
        abuf[r, 16] = zero
    for r in range(4):
        bbuf[r, 16] = zero

    cols_in[0].wait()
    cols_in[1].wait()
    lane = lax.broadcasted_iota(jnp.int32, (1, 128), 1)
    for r in range(5):
        line = jnp.full((1, 128), 16, jnp.int32)
        for k in range(16):
            line = jnp.where(lane == (sac[r, k] if r < 4 else sbc[0, k]), k, line)
        tab[pl.ds(r, 1), :] = line

    full, lo, hi = pl.ds(0, 8), pl.ds(0, 4), pl.ds(4, 4)

    def spread(k):
        for copy in c_in[k]:
            copy.wait_recv()
        mine = ca.at[0, full, chunk[k]]
        return (
            put(mine, ca.at[1, full, chunk[k]], d_yr) if k < 2 else None,
            put(mine, cs.at[0, full, chunk[k]], d_xr),
            put(mine, ca.at[2, full, chunk[k]], d_yl) if k < 2 else None,
            put(mine, cs.at[1, full, chunk[k]], d_xl),
            put(mine, co.at[0, full, chunk[k]], d_co),
        )

    def cols(g, k):
        return pl.ds(4 * k + 2 * ((h + 1 - g) % 2), 2)

    def group_y(g, k):
        src = ca.at[0, cols(g, k), half[1]]
        return (
            put(src, ca.at[1, cols(g, k), half[1]], d_yr),
            put(src, ca.at[2, cols(g, k), half[1]], d_yl),
        )

    def group_right(g, pair):
        pair[0].wait_recv()
        return put(ca.at[1, cols(g, 0), half[1]], ca.at[3, cols(g, 0), half[1]], d_yr)

    def group_left(g, pair):
        pair[1].wait_recv()
        return put(ca.at[2, cols(g, 1), half[1]], ca.at[3, cols(g, 1), half[1]], d_yl)

    def across_x(k, first):
        _, xr, _, xl, _ = first
        xr.wait_recv()
        xr2 = put(cs.at[0, lo, chunk[k]], cs.at[2, lo, chunk[k]], d_xr)
        xl.wait_recv()
        xl2 = put(cs.at[1, hi, chunk[k]], cs.at[2, hi, chunk[k]], d_xl)
        o = put(cs.at[pl.ds(0, 2), full, chunk[k]], co.at[pl.ds(1, 2), full, chunk[k]], d_co)
        return xr2, xl2, o

    def across_y(k, first):
        yr, _, yl, _, _ = first
        yr.wait_recv()
        yr2 = put(ca.at[1, lo, chunk[k]], ca.at[3, lo, chunk[k]], d_yr)
        yl.wait_recv()
        yl2 = put(ca.at[2, hi, chunk[k]], ca.at[3, hi, chunk[k]], d_yl)
        return yr2, yl2

    def last_core(k, second):
        second[0].wait_recv()
        second[1].wait_recv()
        return put(cs.at[2, full, chunk[k]], co.at[3, full, chunk[k]], d_co)

    def dstep(s, half):
        right = (z + 8 - s) % 8
        left = (z + s) % 8
        if half:
            rlo, rhi = pl.ds(0, 256), pl.ds(256, 256)
            return (
                put(dg.at[right, rlo], dg.at[right, rlo], zdev(zr)),
                put(dg.at[left, rhi], dg.at[left, rhi], zdev(zl)),
            )
        return (
            put(dg.at[right], dg.at[right], zdev(zr)),
            put(dg.at[left], dg.at[left], zdev(zl)),
        )

    own_c.wait()
    f0 = spread(0)
    tb_in = [put(tab, ib.at[d], zdev((z + 8 + (2 * l - 1) * d) % 8)) for d in (3, 2, 1)]
    ta_in = put(tab, ia.at[l], zdev(zin))
    own += [move(tab, ia.at[l]), move(tab, ib.at[0])]
    b1.wait_recv()
    b2 = put(bbuf.at[1, quarter], bbuf.at[2, quarter], zdev(zin))
    n0 = across_x(0, f0)
    m0 = across_y(0, f0)
    f1 = spread(1)
    other = 4 * (1 - l)
    a_in.wait_recv()
    piece = abuf.at[other + x, part]
    axr = put(piece, piece, d_xr)
    axl = put(piece, piece, d_xl)
    b2.wait_recv()
    b3 = put(bbuf.at[2, quarter], bbuf.at[3, quarter], zdev(zout))
    dr = put(d_ref, dg.at[z], zdev(zr))
    dl = put(d_ref, dg.at[z], zdev(zl))
    turn(2)
    turn(3)
    o0 = last_core(0, n0)
    b3.wait_recv()
    three = pl.ds(1, 3)
    piece = bbuf.at[three, quarter]
    byr = put(piece, piece, d_yr)
    byl = put(piece, piece, d_yl)
    n1 = across_x(1, f1)
    m1 = across_y(1, f1)
    dr.wait_recv()
    dl.wait_recv()
    dr, dl = dstep(1, False)
    axr.wait_recv()
    piece = abuf.at[other + (x + 3) % 4, pl.ds(8 * c, 4)]
    axr2 = put(piece, piece, d_xr)
    axl.wait_recv()
    piece = abuf.at[other + (x + 1) % 4, pl.ds(8 * c + 4, 4)]
    axl2 = put(piece, piece, d_xl)
    o1 = last_core(1, n1)
    f2 = spread(2)
    axr2.wait_recv()
    axl2.wait_recv()
    piece = abuf.at[pl.ds(other, 4), part]
    a_x = put(piece, piece, d_co)
    byr.wait_recv()
    piece = bbuf.at[three, pl.ds(4 * ((y + 3) % 4), 2)]
    byr2 = put(piece, piece, d_yr)
    byl.wait_recv()
    piece = bbuf.at[three, pl.ds(4 * ((y + 1) % 4) + 2, 2)]
    byl2 = put(piece, piece, d_yl)

    for copy in own:
        copy.wait()
    ta_in.wait_recv()
    for copy in tb_in:
        copy.wait_recv()
    ta_s = move(ia, sa)
    tb_s = move(ib, sb)
    ta_s.wait()
    tb_s.wait()
    a_x.wait_recv()
    ys = [y, (y + 3) % 4, (y + 1) % 4, (y + 2) % 4]

    def fill_a(s):
        def body(t, carry):
            col = ((t // 2 % 2) * 4 + ys[s]) * 4 + (t // 4) * 2 + t % 2
            for r in range(8):
                at = sa[r // 4, r % 4, col]
                ad[s, pl.ds(r * 128, 128), pl.ds(pl.multiple_of(t * 128, 128), 128)] = abuf[r, at]
            return carry

        lax.fori_loop(0, 8, body, 0)

    for s in range(4):
        fill_a(s)

    def alpha_dot(s, k, fresh=False):
        wide = jnp.concatenate(
            [ca[s, pl.ds(2 * q, 2), half[k]].reshape(512, 128) for q in range(4)], axis=1
        )
        res = jnp.dot(ad[s, :, pl.ds(512 * k, 512)], wide, preferred_element_type=F32)
        for q in range(4):
            piece = res[:, q * 128:(q + 1) * 128].reshape(2, 512, 128)
            if fresh:
                acc[pl.ds(2 * q, 2)] = piece
            else:
                acc[pl.ds(2 * q, 2)] += piece

    def alpha_group(s, g):
        wide = jnp.concatenate(
            [ca[s, cols(g, q), half[1]].reshape(512, 128) for q in range(2)], axis=1
        )
        res = jnp.dot(ad[s, :, pl.ds(512, 512)], wide, preferred_element_type=F32)
        for q in range(2):
            acc[cols(g, q)] += res[:, q * 128:(q + 1) * 128].reshape(2, 512, 128)

    near = (h + 3 + 2 * l) % 4
    far = (h + 1 + 2 * l) % 4
    hs = [h, near, far, (h + 2) % 4]
    xs = [x, (x + 3) % 4, (x + 1) % 4, (x + 2) % 4]

    def fill_b(s):
        cc = c if s < 4 else 1 - c
        xx = xs[s % 4]

        def body(t, carry):
            col = (t * 4 + xx) * 2 + cc
            for r in range(4):
                at = sb[r, 4, col]
                rows = pl.ds(pl.multiple_of(hs[r] * 128, 128), 128)
                bd[s, rows, pl.ds(pl.multiple_of(t * 128, 128), 128)] = bbuf[r, at]
            return carry

        lax.fori_loop(0, 4, body, 0)

    def beta_source(s):
        if s == 0:
            return ca.at[0]
        return cs.at[s - 1] if s < 4 else co.at[s - 4]

    def beta_dot(some, k, g=None):
        lhs = jnp.concatenate(
            [beta_source(s)[pl.ds(2 * q, 2), half[k], :].reshape(512, 128) for s in some for q in range(4)],
            axis=1,
        )
        if g is None:
            rhs = [bd[s] for s in some]
            places = [pl.ds(2 * q, 2) for q in range(4)]
        else:
            at = [pl.ds(pl.multiple_of(256 * q + 128 * ((h + 1 - g) % 2), 128), 128) for q in range(2)]
            rhs = [jnp.concatenate([bd[s, rows, :] for rows in at], axis=0) for s in some]
            places = [cols(g, q) for q in range(2)]
        res = lax.dot_general(
            lhs, jnp.concatenate(rhs, axis=1), (((1,), (1,)), ((), ())), preferred_element_type=F32
        )
        for q, place in enumerate(places):
            acc[place, half[k], :] += res[:, q * 128:(q + 1) * 128].reshape(2, 256, 128)

    alpha_dot(0, 0, True)
    alpha_dot(1, 0)
    alpha_dot(2, 0)
    f3 = spread(3)
    g00 = group_y(0, 0)
    g01 = group_y(0, 1)
    g10 = group_y(1, 0)
    for copy in m0 + m1:
        copy.wait_recv()
    alpha_dot(3, 0)
    byr2.wait_recv()
    byl2.wait_recv()
    for s in range(8):
        fill_b(s)
    n2 = across_x(2, f2)
    dr.wait_recv()
    dl.wait_recv()
    dr, dl = dstep(2, False)
    beta_dot((0, 1), 0)
    beta_dot((2, 3), 0)
    n3 = across_x(3, f3)
    r0 = group_right(0, g00)
    l0 = group_left(0, g01)
    g11 = group_y(1, 1)
    f0[4].wait_recv()
    f1[4].wait_recv()
    n0[2].wait_recv()
    n1[2].wait_recv()
    beta_dot((4, 5), 0, 0)
    o0.wait_recv()
    o1.wait_recv()
    beta_dot((6, 7), 0, 0)
    alpha_group(0, 0)
    r1 = group_right(1, g10)
    o2 = last_core(2, n2)
    f2[4].wait_recv()
    f3[4].wait_recv()
    beta_dot((0, 4), 1, 0)
    dr.wait_recv()
    dl.wait_recv()
    dr, dl = dstep(3, True)
    beta_dot((1, 2), 1, 0)
    o3 = last_core(3, n3)
    n2[2].wait_recv()
    n3[2].wait_recv()
    beta_dot((5, 6), 1, 0)
    g01[0].wait_recv()
    alpha_group(1, 0)
    g00[1].wait_recv()
    alpha_group(2, 0)
    r0.wait_recv()
    l0.wait_recv()
    alpha_group(3, 0)
    o2.wait_recv()
    o3.wait_recv()
    beta_dot((3, 7), 1, 0)

    outs = []

    def ready(zz):
        def finish(t, carry):
            rows = pl.ds(pl.multiple_of(t * 128, 128), 128)
            whole = acc[zz, rows] + dg[zz, rows] * ca[0, zz, rows].astype(F32)
            sig[zz, rows] = whole.astype(BF)
            return carry

        lax.fori_loop(0, 4, finish, 0)

    def back(far_h, flip):
        zz = 2 * ((h + far_h) % 4) + (1 - l if flip else l)
        ready(zz)
        outs.append(put(sig.at[zz], out_ref.at[z], zdev(zz)))

    back(1, True)
    back(3, True)
    l1 = group_left(1, g11)
    back(1, False)
    back(3, False)
    beta_dot((4, 5), 0, 1)
    beta_dot((6, 7), 0, 1)
    beta_dot((0, 4), 1, 1)
    beta_dot((1, 2), 1, 1)
    beta_dot((5, 6), 1, 1)
    beta_dot((3, 7), 1, 1)
    alpha_group(0, 1)
    g11[0].wait_recv()
    alpha_group(1, 1)
    g10[1].wait_recv()
    alpha_group(2, 1)
    dr.wait_recv()
    dl.wait_recv()
    r1.wait_recv()
    l1.wait_recv()
    alpha_group(3, 1)
    back(2, False)
    back(2, True)
    back(0, True)
    ready(z)
    last = move(sig.at[z], out_ref.at[z])
    last.wait()
    for copy in outs:
        copy.wait_recv()
    for copy in sent:
        copy.wait_send()


def shards(ci_vectors, alpha_blocks, alpha_cols, beta_blocks, beta_cols, diagonal):
    hbm = pl.BlockSpec(memory_space=pltpu.MemorySpace.HBM)
    return pl.pallas_call(
        kernel,
        out_shape=jax.ShapeDtypeStruct((8, 512, 128), BF),
        in_specs=[hbm] * 6,
        out_specs=hbm,
        scratch_shapes=[
            pltpu.VMEM((4, 8, 512, 128), BF),
            pltpu.VMEM((3, 8, 512, 128), BF),
            pltpu.VMEM((4, 8, 512, 128), BF),
            pltpu.VMEM((8, 17, 128, 128), BF),
            pltpu.VMEM((4, 17, 128, 128), BF),
            pltpu.VMEM((8, 128), jnp.int32),
            pltpu.VMEM((2, 8, 128), jnp.int32),
            pltpu.VMEM((4, 8, 128), jnp.int32),
            pltpu.SMEM((4, 16), jnp.int32),
            pltpu.SMEM((1, 16), jnp.int32),
            pltpu.SMEM((2, 8, 128), jnp.int32),
            pltpu.SMEM((4, 8, 128), jnp.int32),
            pltpu.VMEM((8, 512, 128), F32),
            pltpu.VMEM((4, 1024, 1024), BF),
            pltpu.VMEM((8, 512, 512), BF),
            pltpu.VMEM((8, 512, 128), F32),
            pltpu.VMEM((8, 512, 128), BF),
            pltpu.SemaphoreType.DMA((128,)),
            pltpu.SemaphoreType.DMA((128,)),
            pltpu.SemaphoreType.DMA((16,)),
        ],
        compiler_params=pltpu.CompilerParams(
            collective_id=0, has_side_effects=True, vmem_limit_bytes=60 * 1024 * 1024
        ),
    )(ci_vectors, alpha_blocks, alpha_cols, beta_blocks, beta_cols, diagonal)


def solution(mesh):
    placed = (
        P(None, "alpha", "beta"),
        P("alpha", None, None, None),
        P("alpha", None),
        P("beta", None, None, None),
        P("beta", None),
        P("alpha", "beta"),
    )
    return jax.shard_map(
        shards, mesh=mesh, in_specs=placed, out_specs=P(None, "alpha", "beta"), check_vma=False
    )
```

```python
import jax
import jax.numpy as jnp
from jax import lax
from jax.experimental import pallas as pl
from jax.experimental.pallas import tpu as pltpu
from jax.sharding import PartitionSpec as P

MESH = pl.DeviceIdType.MESH
BF = jnp.bfloat16
F32 = jnp.float32


def kernel(
    c_ref, a_ref, ac_ref, b_ref, bc_ref, d_ref, out_ref,
    ca, cs, co, aown, aoth, bbuf, tab, ia, ib, sac, sbc, sown, soth, sb, dg, ad, bd, acc, sig,
    ss, rs, ls,
):
    i = lax.axis_index("alpha")
    j = lax.axis_index("beta")
    l = i // 4
    y = i % 4
    c = j % 2
    x = (j // 2) % 4
    h = j // 8
    z = 2 * h + l

    def dev(xx, yy, zz, cc):
        return ((zz % 2) * 4 + yy, ((zz // 2) * 4 + xx) * 2 + cc)

    def zdev(zz):
        return dev(x, y, zz, c)

    zr = (z + 1) % 8
    zl = (z + 7) % 8
    zin = 2 * h + (1 - l)
    zout = (z + 7 + 2 * l) % 8
    d_xr = dev((x + 1) % 4, y, z, c)
    d_xl = dev((x + 3) % 4, y, z, c)
    d_yr = dev(x, (y + 1) % 4, z, c)
    d_yl = dev(x, (y + 3) % 4, z, c)
    d_co = dev(x, y, z, 1 - c)

    barrier = pltpu.get_barrier_semaphore()
    peers = [zdev((z + d) % 8) for d in range(1, 8)] + [d_xr, d_xl, d_yr, d_yl, d_co]
    for p in peers:
        pl.semaphore_signal(barrier, inc=1, device_id=p, device_id_type=MESH)
    pl.semaphore_wait(barrier, len(peers))

    count = [0]
    sent = []

    def put(src, dst, device):
        k = count[0]
        count[0] += 1
        copy = pltpu.make_async_remote_copy(
            src_ref=src, dst_ref=dst, send_sem=ss.at[k], recv_sem=rs.at[k],
            device_id=device, device_id_type=MESH,
        )
        copy.start()
        sent.append(copy)
        return copy

    lcount = [0]

    def move(src, dst):
        k = lcount[0]
        lcount[0] += 1
        copy = pltpu.make_async_copy(src, dst, ls.at[k])
        copy.start()
        return copy

    cols_in = [move(ac_ref, sac), move(bc_ref, sbc)]
    chunk = [pl.ds(128 * k, 128) for k in range(4)]
    half = (pl.ds(0, 256), pl.ds(256, 256))
    own_c = move(c_ref.at[z], ca.at[0, z])
    c_in = ([], [], [], [])

    def turn(k):
        for d in (4, 3, 5, 2, 6, 1, 7):
            zz = (z + d) % 8
            c_in[k].append(put(c_ref.at[zz, chunk[k]], ca.at[0, z, chunk[k]], zdev(zz)))

    quarter = pl.ds(4 * y, 4)
    part = pl.ds(8 * c, 8)
    turn(0)
    b1 = put(b_ref.at[0, quarter], bbuf.at[1, quarter], zdev(zout))
    turn(1)
    a_in = put(a_ref.at[x, part], aoth.at[x, part], zdev(jnp.where(c == 0, zin, zout)))
    own = [
        move(a_ref.at[r], aown.at[r, pl.ds(0, 16)]) for r in range(4)
    ] + [
        move(b_ref.at[0], bbuf.at[0, pl.ds(0, 16)]),
        move(d_ref, dg.at[z]),
    ]
    zero = jnp.zeros((128, 128), BF)
    for r in range(4):
        aown[r, 16] = zero
        aoth[r, 16] = zero
        bbuf[r, 16] = zero

    cols_in[0].wait()
    cols_in[1].wait()
    lane = lax.broadcasted_iota(jnp.int32, (1, 128), 1)
    for r in range(5):
        line = jnp.full((1, 128), 16, jnp.int32)
        for k in range(16):
            line = jnp.where(lane == (sac[r, k] if r < 4 else sbc[0, k]), k, line)
        tab[pl.ds(r, 1), :] = line

    full, lo, hi = pl.ds(0, 8), pl.ds(0, 4), pl.ds(4, 4)

    def spread(k):
        for copy in c_in[k]:
            copy.wait_recv()
        mine = ca.at[0, full, chunk[k]]
        return (
            put(mine, ca.at[1, full, chunk[k]], d_yr) if k < 2 else None,
            put(mine, cs.at[0, full, chunk[k]], d_xr),
            put(mine, ca.at[2, full, chunk[k]], d_yl) if k < 2 else None,
            put(mine, cs.at[1, full, chunk[k]], d_xl),
            put(mine, co.at[0, full, chunk[k]], d_co),
        )

    def cols(g, k):
        return pl.ds(4 * k + 2 * ((h + 1 - g) % 2), 2)

    def group_y(g, k):
        src = ca.at[0, cols(g, k), half[1]]
        return (
            put(src, ca.at[1, cols(g, k), half[1]], d_yr),
            put(src, ca.at[2, cols(g, k), half[1]], d_yl),
        )

    def group_right(g, pair):
        pair[0].wait_recv()
        return put(ca.at[1, cols(g, 0), half[1]], ca.at[3, cols(g, 0), half[1]], d_yr)

    def group_left(g, pair):
        pair[1].wait_recv()
        return put(ca.at[2, cols(g, 1), half[1]], ca.at[3, cols(g, 1), half[1]], d_yl)

    def across_x(k, first):
        _, xr, _, xl, _ = first
        xr.wait_recv()
        xr2 = put(cs.at[0, lo, chunk[k]], cs.at[2, lo, chunk[k]], d_xr)
        xl.wait_recv()
        xl2 = put(cs.at[1, hi, chunk[k]], cs.at[2, hi, chunk[k]], d_xl)
        o = put(cs.at[pl.ds(0, 2), full, chunk[k]], co.at[pl.ds(1, 2), full, chunk[k]], d_co)
        return xr2, xl2, o

    def across_y(k, first):
        yr, _, yl, _, _ = first
        yr.wait_recv()
        yr2 = put(ca.at[1, lo, chunk[k]], ca.at[3, lo, chunk[k]], d_yr)
        yl.wait_recv()
        yl2 = put(ca.at[2, hi, chunk[k]], ca.at[3, hi, chunk[k]], d_yl)
        return yr2, yl2

    def last_core(k, second):
        second[0].wait_recv()
        second[1].wait_recv()
        return put(cs.at[2, full, chunk[k]], co.at[3, full, chunk[k]], d_co)

    def dstep(s, half):
        right = (z + 8 - s) % 8
        left = (z + s) % 8
        if half:
            rlo, rhi = pl.ds(0, 256), pl.ds(256, 256)
            return (
                put(dg.at[right, rlo], dg.at[right, rlo], zdev(zr)),
                put(dg.at[left, rhi], dg.at[left, rhi], zdev(zl)),
            )
        return (
            put(dg.at[right], dg.at[right], zdev(zr)),
            put(dg.at[left], dg.at[left], zdev(zl)),
        )

    ys = [y, (y + 3) % 4, (y + 1) % 4, (y + 2) % 4]

    def fill_a(s, blocks, table, low):
        def body(t, carry):
            col = ((t // 2 % 2) * 4 + ys[s]) * 4 + (t // 4) * 2 + t % 2
            for r in range(4):
                at = table[r, col]
                rows = pl.ds(pl.multiple_of(low * 512 + r * 128, 128), 128)
                ad[s, rows, pl.ds(pl.multiple_of(t * 128, 128), 128)] = blocks[r, at]
            return carry

        lax.fori_loop(0, 8, body, 0)

    def alpha_dot(some, low, fresh):
        wide = jnp.concatenate(
            [
                jnp.concatenate(
                    [ca[s, pl.ds(2 * q, 2), half[0]].reshape(512, 128) for q in range(4)], axis=1
                )
                for s in some
            ],
            axis=0,
        )
        rows = pl.ds(pl.multiple_of(low * 512, 512), 512)
        lhs = jnp.concatenate([ad[s, rows, pl.ds(0, 512)] for s in some], axis=1)
        res = jnp.dot(lhs, wide, preferred_element_type=F32)
        for q in range(4):
            piece = res[:, q * 128:(q + 1) * 128]
            if fresh:
                acc[2 * q + low] = piece
            else:
                acc[2 * q + low] += piece

    own_c.wait()
    f0 = spread(0)
    tb_in = [put(tab, ib.at[d], zdev((z + 8 + (2 * l - 1) * d) % 8)) for d in (3, 2, 1)]
    ta_in = put(tab, ia, zdev(zin))
    tab_own = move(tab, sown)
    own.append(move(tab, ib.at[0]))
    b1.wait_recv()
    b2 = put(bbuf.at[1, quarter], bbuf.at[2, quarter], zdev(zin))
    n0 = across_x(0, f0)
    m0 = across_y(0, f0)
    f1 = spread(1)
    a_in.wait_recv()
    piece = aoth.at[x, part]
    axr = put(piece, piece, d_xr)
    axl = put(piece, piece, d_xl)
    b2.wait_recv()
    b3 = put(bbuf.at[2, quarter], bbuf.at[3, quarter], zdev(zout))
    dr = put(d_ref, dg.at[z], zdev(zr))
    dl = put(d_ref, dg.at[z], zdev(zl))
    turn(2)
    turn(3)
    o0 = last_core(0, n0)
    b3.wait_recv()
    three = pl.ds(1, 3)
    piece = bbuf.at[three, quarter]
    byr = put(piece, piece, d_yr)
    byl = put(piece, piece, d_yl)
    n1 = across_x(1, f1)
    m1 = across_y(1, f1)
    for copy in own[:4]:
        copy.wait()
    tab_own.wait()
    for s in range(4):
        fill_a(s, aown, sown, l)
    dr.wait_recv()
    dl.wait_recv()
    dr, dl = dstep(1, False)
    axr.wait_recv()
    piece = aoth.at[(x + 3) % 4, pl.ds(8 * c, 4)]
    axr2 = put(piece, piece, d_xr)
    axl.wait_recv()
    piece = aoth.at[(x + 1) % 4, pl.ds(8 * c + 4, 4)]
    axl2 = put(piece, piece, d_xl)
    alpha_dot((0, 1, 2), l, True)
    o1 = last_core(1, n1)
    f2 = spread(2)
    axr2.wait_recv()
    axl2.wait_recv()
    piece = aoth.at[pl.ds(0, 4), part]
    a_x = put(piece, piece, d_co)
    byr.wait_recv()
    piece = bbuf.at[three, pl.ds(4 * ((y + 3) % 4), 2)]
    byr2 = put(piece, piece, d_yr)
    byl.wait_recv()
    piece = bbuf.at[three, pl.ds(4 * ((y + 1) % 4) + 2, 2)]
    byl2 = put(piece, piece, d_yl)

    for copy in own[4:]:
        copy.wait()
    ta_in.wait_recv()
    for copy in tb_in:
        copy.wait_recv()
    ta_s = move(ia, soth)
    tb_s = move(ib, sb)
    ta_s.wait()
    tb_s.wait()
    a_x.wait_recv()
    def alpha_group(s, g):
        wide = jnp.concatenate(
            [ca[s, cols(g, q), half[1]].reshape(512, 128) for q in range(2)], axis=1
        )
        res = jnp.dot(ad[s, :, pl.ds(512, 512)], wide, preferred_element_type=F32)
        for q in range(2):
            acc[cols(g, q)] += res[:, q * 128:(q + 1) * 128].reshape(2, 512, 128)

    near = (h + 3 + 2 * l) % 4
    far = (h + 1 + 2 * l) % 4
    hs = [h, near, far, (h + 2) % 4]
    xs = [x, (x + 3) % 4, (x + 1) % 4, (x + 2) % 4]

    def fill_b(s):
        cc = c if s < 4 else 1 - c
        xx = xs[s % 4]

        def body(t, carry):
            col = (t * 4 + xx) * 2 + cc
            for r in range(4):
                at = sb[r, 4, col]
                rows = pl.ds(pl.multiple_of(hs[r] * 128, 128), 128)
                bd[s, rows, pl.ds(pl.multiple_of(t * 128, 128), 128)] = bbuf[r, at]
            return carry

        lax.fori_loop(0, 4, body, 0)

    def beta_source(s):
        if s == 0:
            return ca.at[0]
        return cs.at[s - 1] if s < 4 else co.at[s - 4]

    def beta_dot(some, k, g=None):
        lhs = jnp.concatenate(
            [beta_source(s)[pl.ds(2 * q, 2), half[k], :].reshape(512, 128) for s in some for q in range(4)],
            axis=1,
        )
        if g is None:
            rhs = [bd[s] for s in some]
            places = [pl.ds(2 * q, 2) for q in range(4)]
        else:
            at = [pl.ds(pl.multiple_of(256 * q + 128 * ((h + 1 - g) % 2), 128), 128) for q in range(2)]
            rhs = [jnp.concatenate([bd[s, rows, :] for rows in at], axis=0) for s in some]
            places = [cols(g, q) for q in range(2)]
        res = lax.dot_general(
            lhs, jnp.concatenate(rhs, axis=1), (((1,), (1,)), ((), ())), preferred_element_type=F32
        )
        for q, place in enumerate(places):
            acc[place, half[k], :] += res[:, q * 128:(q + 1) * 128].reshape(2, 256, 128)

    for s in range(4):
        fill_a(s, aoth, soth, 1 - l)
    alpha_dot((0, 1, 2), 1 - l, True)
    f3 = spread(3)
    g00 = group_y(0, 0)
    g01 = group_y(0, 1)
    g10 = group_y(1, 0)
    for copy in m0 + m1:
        copy.wait_recv()
    alpha_dot((3,), l, False)
    alpha_dot((3,), 1 - l, False)
    byr2.wait_recv()
    byl2.wait_recv()
    for s in range(8):
        fill_b(s)
    n2 = across_x(2, f2)
    dr.wait_recv()
    dl.wait_recv()
    dr, dl = dstep(2, False)
    beta_dot((0, 1), 0)
    beta_dot((2, 3), 0)
    n3 = across_x(3, f3)
    r0 = group_right(0, g00)
    l0 = group_left(0, g01)
    g11 = group_y(1, 1)
    f0[4].wait_recv()
    f1[4].wait_recv()
    n0[2].wait_recv()
    n1[2].wait_recv()
    beta_dot((4, 5), 0, 0)
    o0.wait_recv()
    o1.wait_recv()
    beta_dot((6, 7), 0, 0)
    alpha_group(0, 0)
    r1 = group_right(1, g10)
    o2 = last_core(2, n2)
    f2[4].wait_recv()
    f3[4].wait_recv()
    beta_dot((0, 4), 1, 0)
    dr.wait_recv()
    dl.wait_recv()
    dr, dl = dstep(3, True)
    beta_dot((1, 2), 1, 0)
    o3 = last_core(3, n3)
    n2[2].wait_recv()
    n3[2].wait_recv()
    beta_dot((5, 6), 1, 0)
    g01[0].wait_recv()
    alpha_group(1, 0)
    g00[1].wait_recv()
    alpha_group(2, 0)
    r0.wait_recv()
    l0.wait_recv()
    alpha_group(3, 0)
    o2.wait_recv()
    o3.wait_recv()
    beta_dot((3, 7), 1, 0)

    outs = []

    def ready(zz):
        def finish(t, carry):
            rows = pl.ds(pl.multiple_of(t * 128, 128), 128)
            whole = acc[zz, rows] + dg[zz, rows] * ca[0, zz, rows].astype(F32)
            sig[zz, rows] = whole.astype(BF)
            return carry

        lax.fori_loop(0, 4, finish, 0)

    def back(far_h, flip):
        zz = 2 * ((h + far_h) % 4) + (1 - l if flip else l)
        ready(zz)
        outs.append(put(sig.at[zz], out_ref.at[z], zdev(zz)))

    back(1, True)
    back(3, True)
    l1 = group_left(1, g11)
    back(1, False)
    back(3, False)
    beta_dot((4, 5), 0, 1)
    beta_dot((6, 7), 0, 1)
    beta_dot((0, 4), 1, 1)
    beta_dot((1, 2), 1, 1)
    beta_dot((5, 6), 1, 1)
    beta_dot((3, 7), 1, 1)
    alpha_group(0, 1)
    g11[0].wait_recv()
    alpha_group(1, 1)
    g10[1].wait_recv()
    alpha_group(2, 1)
    dr.wait_recv()
    dl.wait_recv()
    r1.wait_recv()
    l1.wait_recv()
    alpha_group(3, 1)
    back(2, False)
    back(2, True)
    back(0, True)
    ready(z)
    last = move(sig.at[z], out_ref.at[z])
    last.wait()
    for copy in outs:
        copy.wait_recv()
    for copy in sent:
        copy.wait_send()


def shards(ci_vectors, alpha_blocks, alpha_cols, beta_blocks, beta_cols, diagonal):
    hbm = pl.BlockSpec(memory_space=pltpu.MemorySpace.HBM)
    return pl.pallas_call(
        kernel,
        out_shape=jax.ShapeDtypeStruct((8, 512, 128), BF),
        in_specs=[hbm] * 6,
        out_specs=hbm,
        scratch_shapes=[
            pltpu.VMEM((4, 8, 512, 128), BF),
            pltpu.VMEM((3, 8, 512, 128), BF),
            pltpu.VMEM((4, 8, 512, 128), BF),
            pltpu.VMEM((4, 17, 128, 128), BF),
            pltpu.VMEM((4, 17, 128, 128), BF),
            pltpu.VMEM((4, 17, 128, 128), BF),
            pltpu.VMEM((8, 128), jnp.int32),
            pltpu.VMEM((8, 128), jnp.int32),
            pltpu.VMEM((4, 8, 128), jnp.int32),
            pltpu.SMEM((4, 16), jnp.int32),
            pltpu.SMEM((1, 16), jnp.int32),
            pltpu.SMEM((8, 128), jnp.int32),
            pltpu.SMEM((8, 128), jnp.int32),
            pltpu.SMEM((4, 8, 128), jnp.int32),
            pltpu.VMEM((8, 512, 128), F32),
            pltpu.VMEM((4, 1024, 1024), BF),
            pltpu.VMEM((8, 512, 512), BF),
            pltpu.VMEM((8, 512, 128), F32),
            pltpu.VMEM((8, 512, 128), BF),
            pltpu.SemaphoreType.DMA((128,)),
            pltpu.SemaphoreType.DMA((128,)),
            pltpu.SemaphoreType.DMA((16,)),
        ],
        compiler_params=pltpu.CompilerParams(
            collective_id=0, has_side_effects=True, vmem_limit_bytes=60 * 1024 * 1024
        ),
    )(ci_vectors, alpha_blocks, alpha_cols, beta_blocks, beta_cols, diagonal)


def solution(mesh):
    placed = (
        P(None, "alpha", "beta"),
        P("alpha", None, None, None),
        P("alpha", None),
        P("beta", None, None, None),
        P("beta", None),
        P("alpha", "beta"),
    )
    return jax.shard_map(
        shards, mesh=mesh, in_specs=placed, out_specs=P(None, "alpha", "beta"), check_vma=False
    )
```

```python
import jax
import jax.numpy as jnp
from jax import lax
from jax.experimental import pallas as pl
from jax.experimental.pallas import tpu as pltpu
from jax.sharding import PartitionSpec as P

MESH = pl.DeviceIdType.MESH
BF = jnp.bfloat16
F32 = jnp.float32


def kernel(
    c_ref, a_ref, ac_ref, b_ref, bc_ref, d_ref, out_ref,
    ca, cs, co, aown, aoth, bbuf, tab, ia, ib, sac, sbc, sown, soth, sb, dg, ad, bd, acc, sig,
    ss, rs, ls,
):
    i = lax.axis_index("alpha")
    j = lax.axis_index("beta")
    l = i // 4
    y = i % 4
    c = j % 2
    x = (j // 2) % 4
    h = j // 8
    z = 2 * h + l

    def dev(xx, yy, zz, cc):
        return ((zz % 2) * 4 + yy, ((zz // 2) * 4 + xx) * 2 + cc)

    def zdev(zz):
        return dev(x, y, zz, c)

    zr = (z + 1) % 8
    zl = (z + 7) % 8
    zin = 2 * h + (1 - l)
    zout = (z + 7 + 2 * l) % 8
    d_xr = dev((x + 1) % 4, y, z, c)
    d_xl = dev((x + 3) % 4, y, z, c)
    d_yr = dev(x, (y + 1) % 4, z, c)
    d_yl = dev(x, (y + 3) % 4, z, c)
    d_co = dev(x, y, z, 1 - c)

    barrier = pltpu.get_barrier_semaphore()
    peers = [zdev((z + d) % 8) for d in range(1, 8)] + [d_xr, d_xl, d_yr, d_yl, d_co]
    for p in peers:
        pl.semaphore_signal(barrier, inc=1, device_id=p, device_id_type=MESH)
    pl.semaphore_wait(barrier, len(peers))

    count = [0]
    sent = []

    def put(src, dst, device):
        k = count[0]
        count[0] += 1
        copy = pltpu.make_async_remote_copy(
            src_ref=src, dst_ref=dst, send_sem=ss.at[k], recv_sem=rs.at[k],
            device_id=device, device_id_type=MESH,
        )
        copy.start()
        sent.append(copy)
        return copy

    lcount = [0]

    def move(src, dst):
        k = lcount[0]
        lcount[0] += 1
        copy = pltpu.make_async_copy(src, dst, ls.at[k])
        copy.start()
        return copy

    cols_in = [move(ac_ref, sac), move(bc_ref, sbc)]
    chunk = [pl.ds(128 * k, 128) for k in range(4)]
    half = (pl.ds(0, 256), pl.ds(256, 256))
    own_c = move(c_ref.at[z], ca.at[0, z])
    c_in = ([], [], [], [])

    def turn(k):
        for d in (4, 3, 5, 2, 6, 1, 7):
            zz = (z + d) % 8
            c_in[k].append(put(c_ref.at[zz, chunk[k]], ca.at[0, z, chunk[k]], zdev(zz)))

    quarter = pl.ds(4 * y, 4)
    part = pl.ds(8 * c, 8)
    turn(0)
    b1 = put(b_ref.at[0, quarter], bbuf.at[1, quarter], zdev(zout))
    turn(1)
    a_in = put(a_ref.at[x, part], aoth.at[x, part], zdev(jnp.where(c == 0, zin, zout)))
    own = [
        move(a_ref.at[r], aown.at[r, pl.ds(0, 16)]) for r in range(4)
    ] + [
        move(b_ref.at[0], bbuf.at[0, pl.ds(0, 16)]),
        move(d_ref, dg.at[z]),
    ]
    zero = jnp.zeros((128, 128), BF)
    for r in range(4):
        aown[r, 16] = zero
        aoth[r, 16] = zero
        bbuf[r, 16] = zero

    cols_in[0].wait()
    cols_in[1].wait()
    lane = lax.broadcasted_iota(jnp.int32, (1, 128), 1)
    for r in range(5):
        line = jnp.full((1, 128), 16, jnp.int32)
        for k in range(16):
            line = jnp.where(lane == (sac[r, k] if r < 4 else sbc[0, k]), k, line)
        tab[pl.ds(r, 1), :] = line

    full, lo, hi = pl.ds(0, 8), pl.ds(0, 4), pl.ds(4, 4)

    def spread(k):
        for copy in c_in[k]:
            copy.wait_recv()
        mine = ca.at[0, full, chunk[k]]
        return (
            put(mine, ca.at[1, full, chunk[k]], d_yr) if k < 2 else None,
            put(mine, cs.at[0, full, chunk[k]], d_xr),
            put(mine, ca.at[2, full, chunk[k]], d_yl) if k < 2 else None,
            put(mine, cs.at[1, full, chunk[k]], d_xl),
            put(mine, co.at[0, full, chunk[k]], d_co),
        )

    def cols(g, k):
        return pl.ds(4 * k + 2 * ((h + 1 - g) % 2), 2)

    def group_y(g, k):
        src = ca.at[0, cols(g, k), half[1]]
        return (
            put(src, ca.at[1, cols(g, k), half[1]], d_yr),
            put(src, ca.at[2, cols(g, k), half[1]], d_yl),
        )

    def group_right(g, pair):
        pair[0].wait_recv()
        return put(ca.at[1, cols(g, 0), half[1]], ca.at[3, cols(g, 0), half[1]], d_yr)

    def group_left(g, pair):
        pair[1].wait_recv()
        return put(ca.at[2, cols(g, 1), half[1]], ca.at[3, cols(g, 1), half[1]], d_yl)

    def across_x(k, first):
        _, xr, _, xl, _ = first
        xr.wait_recv()
        xr2 = put(cs.at[0, lo, chunk[k]], cs.at[2, lo, chunk[k]], d_xr)
        xl.wait_recv()
        xl2 = put(cs.at[1, hi, chunk[k]], cs.at[2, hi, chunk[k]], d_xl)
        o = put(cs.at[pl.ds(0, 2), full, chunk[k]], co.at[pl.ds(1, 2), full, chunk[k]], d_co)
        return xr2, xl2, o

    def across_y(k, first):
        yr, _, yl, _, _ = first
        yr.wait_recv()
        yr2 = put(ca.at[1, lo, chunk[k]], ca.at[3, lo, chunk[k]], d_yr)
        yl.wait_recv()
        yl2 = put(ca.at[2, hi, chunk[k]], ca.at[3, hi, chunk[k]], d_yl)
        return yr2, yl2

    def last_core(k, second):
        second[0].wait_recv()
        second[1].wait_recv()
        return put(cs.at[2, full, chunk[k]], co.at[3, full, chunk[k]], d_co)

    def dstep(s, half):
        right = (z + 8 - s) % 8
        left = (z + s) % 8
        if half:
            rlo, rhi = pl.ds(0, 256), pl.ds(256, 256)
            return (
                put(dg.at[right, rlo], dg.at[right, rlo], zdev(zr)),
                put(dg.at[left, rhi], dg.at[left, rhi], zdev(zl)),
            )
        return (
            put(dg.at[right], dg.at[right], zdev(zr)),
            put(dg.at[left], dg.at[left], zdev(zl)),
        )

    ys = [y, (y + 3) % 4, (y + 1) % 4, (y + 2) % 4]

    def fill_a(s, blocks, table, low):
        def body(t, carry):
            col = ((t // 2 % 2) * 4 + ys[s]) * 4 + (t // 4) * 2 + t % 2
            for r in range(4):
                at = table[r, col]
                rows = pl.ds(pl.multiple_of(low * 512 + r * 128, 128), 128)
                ad[s, rows, pl.ds(pl.multiple_of(t * 128, 128), 128)] = blocks[r, at]
            return carry

        lax.fori_loop(0, 8, body, 0)

    def alpha_dot(some, low, fresh):
        wide = jnp.concatenate(
            [
                jnp.concatenate(
                    [ca[s, pl.ds(2 * q, 2), half[0]].reshape(512, 128) for q in range(4)], axis=1
                )
                for s in some
            ],
            axis=0,
        )
        rows = pl.ds(pl.multiple_of(low * 512, 512), 512)
        lhs = jnp.concatenate([ad[s, rows, pl.ds(0, 512)] for s in some], axis=1)
        res = jnp.dot(lhs, wide, preferred_element_type=F32)
        for q in range(4):
            piece = res[:, q * 128:(q + 1) * 128]
            if fresh:
                acc[2 * q + low] = piece
            else:
                acc[2 * q + low] += piece

    own_c.wait()
    f0 = spread(0)
    tb_in = [put(tab, ib.at[d], zdev((z + 8 + (2 * l - 1) * d) % 8)) for d in (3, 2, 1)]
    ta_in = put(tab, ia, zdev(zin))
    tab_own = move(tab, sown)
    own.append(move(tab, ib.at[0]))
    b1.wait_recv()
    b2 = put(bbuf.at[1, quarter], bbuf.at[2, quarter], zdev(zin))
    n0 = across_x(0, f0)
    m0 = across_y(0, f0)
    f1 = spread(1)
    a_in.wait_recv()
    piece = aoth.at[x, part]
    axr = put(piece, piece, d_xr)
    axl = put(piece, piece, d_xl)
    b2.wait_recv()
    b3 = put(bbuf.at[2, quarter], bbuf.at[3, quarter], zdev(zout))
    dr = put(d_ref, dg.at[z], zdev(zr))
    dl = put(d_ref, dg.at[z], zdev(zl))
    turn(2)
    turn(3)
    o0 = last_core(0, n0)
    b3.wait_recv()
    three = pl.ds(1, 3)
    piece = bbuf.at[three, quarter]
    byr = put(piece, piece, d_yr)
    byl = put(piece, piece, d_yl)
    n1 = across_x(1, f1)
    m1 = across_y(1, f1)
    for copy in own[:4]:
        copy.wait()
    tab_own.wait()
    for s in range(4):
        fill_a(s, aown, sown, l)
    dr.wait_recv()
    dl.wait_recv()
    dr, dl = dstep(1, False)
    axr.wait_recv()
    piece = aoth.at[(x + 3) % 4, pl.ds(8 * c, 4)]
    axr2 = put(piece, piece, d_xr)
    axl.wait_recv()
    piece = aoth.at[(x + 1) % 4, pl.ds(8 * c + 4, 4)]
    axl2 = put(piece, piece, d_xl)
    alpha_dot((0, 1, 2), l, True)
    o1 = last_core(1, n1)
    f2 = spread(2)
    axr2.wait_recv()
    axl2.wait_recv()
    piece = aoth.at[pl.ds(0, 4), part]
    a_x = put(piece, piece, d_co)
    byr.wait_recv()
    piece = bbuf.at[three, pl.ds(4 * ((y + 3) % 4), 2)]
    byr2 = put(piece, piece, d_yr)
    byl.wait_recv()
    piece = bbuf.at[three, pl.ds(4 * ((y + 1) % 4) + 2, 2)]
    byl2 = put(piece, piece, d_yl)

    for copy in own[4:]:
        copy.wait()
    ta_in.wait_recv()
    for copy in tb_in:
        copy.wait_recv()
    ta_s = move(ia, soth)
    tb_s = move(ib, sb)
    ta_s.wait()
    tb_s.wait()
    a_x.wait_recv()
    def alpha_group(s, g):
        wide = jnp.concatenate(
            [ca[s, cols(g, q), half[1]].reshape(512, 128) for q in range(2)], axis=1
        )
        res = jnp.dot(ad[s, :, pl.ds(512, 512)], wide, preferred_element_type=F32)
        for q in range(2):
            acc[cols(g, q)] += res[:, q * 128:(q + 1) * 128].reshape(2, 512, 128)

    near = (h + 3 + 2 * l) % 4
    far = (h + 1 + 2 * l) % 4
    hs = [h, near, far, (h + 2) % 4]
    xs = [x, (x + 3) % 4, (x + 1) % 4, (x + 2) % 4]

    def fill_b(s):
        cc = c if s < 4 else 1 - c
        xx = xs[s % 4]

        def body(t, carry):
            col = (t * 4 + xx) * 2 + cc
            for r in range(4):
                at = sb[r, 4, col]
                rows = pl.ds(pl.multiple_of(hs[r] * 128, 128), 128)
                bd[s, rows, pl.ds(pl.multiple_of(t * 128, 128), 128)] = bbuf[r, at]
            return carry

        lax.fori_loop(0, 4, body, 0)

    def beta_source(s):
        if s == 0:
            return ca.at[0]
        return cs.at[s - 1] if s < 4 else co.at[s - 4]

    def beta_dot(some, k, g=None):
        lhs = jnp.concatenate(
            [beta_source(s)[pl.ds(2 * q, 2), half[k], :].reshape(512, 128) for s in some for q in range(4)],
            axis=1,
        )
        if g is None:
            rhs = [bd[s] for s in some]
            places = [pl.ds(2 * q, 2) for q in range(4)]
        else:
            at = [pl.ds(pl.multiple_of(256 * q + 128 * ((h + 1 - g) % 2), 128), 128) for q in range(2)]
            rhs = [jnp.concatenate([bd[s, rows, :] for rows in at], axis=0) for s in some]
            places = [cols(g, q) for q in range(2)]
        res = lax.dot_general(
            lhs, jnp.concatenate(rhs, axis=1), (((1,), (1,)), ((), ())), preferred_element_type=F32
        )
        for q, place in enumerate(places):
            acc[place, half[k], :] += res[:, q * 128:(q + 1) * 128].reshape(2, 256, 128)

    for s in range(4):
        fill_a(s, aoth, soth, 1 - l)
    alpha_dot((0, 1, 2), 1 - l, True)
    f3 = spread(3)
    g00 = group_y(0, 0)
    g01 = group_y(0, 1)
    g10 = group_y(1, 0)
    for copy in m0 + m1:
        copy.wait_recv()
    alpha_dot((3,), l, False)
    alpha_dot((3,), 1 - l, False)
    byr2.wait_recv()
    byl2.wait_recv()
    for s in range(8):
        fill_b(s)
    n2 = across_x(2, f2)
    dr.wait_recv()
    dl.wait_recv()
    dr, dl = dstep(2, False)
    beta_dot((0, 1), 0)
    r0 = group_right(0, g00)
    l0 = group_left(0, g01)
    g11 = group_y(1, 1)
    beta_dot((2, 3), 0)
    n3 = across_x(3, f3)
    f0[4].wait_recv()
    f1[4].wait_recv()
    n0[2].wait_recv()
    n1[2].wait_recv()
    beta_dot((4, 5), 0, 0)
    o0.wait_recv()
    o1.wait_recv()
    beta_dot((6, 7), 0, 0)
    alpha_group(0, 0)
    r1 = group_right(1, g10)
    o2 = last_core(2, n2)
    f2[4].wait_recv()
    f3[4].wait_recv()
    beta_dot((0, 4), 1, 0)
    dr.wait_recv()
    dl.wait_recv()
    dr, dl = dstep(3, True)
    beta_dot((1, 2), 1, 0)
    o3 = last_core(3, n3)
    n2[2].wait_recv()
    n3[2].wait_recv()
    beta_dot((5, 6), 1, 0)
    g01[0].wait_recv()
    alpha_group(1, 0)
    g00[1].wait_recv()
    alpha_group(2, 0)
    r0.wait_recv()
    l0.wait_recv()
    alpha_group(3, 0)
    o2.wait_recv()
    o3.wait_recv()
    beta_dot((3, 7), 1, 0)

    outs = []

    def ready(zz):
        def finish(t, carry):
            rows = pl.ds(pl.multiple_of(t * 128, 128), 128)
            whole = acc[zz, rows] + dg[zz, rows] * ca[0, zz, rows].astype(F32)
            sig[zz, rows] = whole.astype(BF)
            return carry

        lax.fori_loop(0, 4, finish, 0)

    def back(far_h, flip):
        zz = 2 * ((h + far_h) % 4) + (1 - l if flip else l)
        ready(zz)
        outs.append(put(sig.at[zz], out_ref.at[z], zdev(zz)))

    back(1, True)
    back(3, True)
    l1 = group_left(1, g11)
    back(1, False)
    back(3, False)
    beta_dot((4, 5), 0, 1)
    beta_dot((6, 7), 0, 1)
    beta_dot((0, 4), 1, 1)
    beta_dot((1, 2), 1, 1)
    beta_dot((5, 6), 1, 1)
    beta_dot((3, 7), 1, 1)
    alpha_group(0, 1)
    g11[0].wait_recv()
    alpha_group(1, 1)
    g10[1].wait_recv()
    alpha_group(2, 1)
    dr.wait_recv()
    dl.wait_recv()
    r1.wait_recv()
    l1.wait_recv()
    alpha_group(3, 1)
    back(2, False)
    back(2, True)
    back(0, True)
    ready(z)
    last = move(sig.at[z], out_ref.at[z])
    last.wait()
    for copy in outs:
        copy.wait_recv()
    for copy in sent:
        copy.wait_send()


def shards(ci_vectors, alpha_blocks, alpha_cols, beta_blocks, beta_cols, diagonal):
    hbm = pl.BlockSpec(memory_space=pltpu.MemorySpace.HBM)
    return pl.pallas_call(
        kernel,
        out_shape=jax.ShapeDtypeStruct((8, 512, 128), BF),
        in_specs=[hbm] * 6,
        out_specs=hbm,
        scratch_shapes=[
            pltpu.VMEM((4, 8, 512, 128), BF),
            pltpu.VMEM((3, 8, 512, 128), BF),
            pltpu.VMEM((4, 8, 512, 128), BF),
            pltpu.VMEM((4, 17, 128, 128), BF),
            pltpu.VMEM((4, 17, 128, 128), BF),
            pltpu.VMEM((4, 17, 128, 128), BF),
            pltpu.VMEM((8, 128), jnp.int32),
            pltpu.VMEM((8, 128), jnp.int32),
            pltpu.VMEM((4, 8, 128), jnp.int32),
            pltpu.SMEM((4, 16), jnp.int32),
            pltpu.SMEM((1, 16), jnp.int32),
            pltpu.SMEM((8, 128), jnp.int32),
            pltpu.SMEM((8, 128), jnp.int32),
            pltpu.SMEM((4, 8, 128), jnp.int32),
            pltpu.VMEM((8, 512, 128), F32),
            pltpu.VMEM((4, 1024, 1024), BF),
            pltpu.VMEM((8, 512, 512), BF),
            pltpu.VMEM((8, 512, 128), F32),
            pltpu.VMEM((8, 512, 128), BF),
            pltpu.SemaphoreType.DMA((128,)),
            pltpu.SemaphoreType.DMA((128,)),
            pltpu.SemaphoreType.DMA((16,)),
        ],
        compiler_params=pltpu.CompilerParams(
            collective_id=0, has_side_effects=True, vmem_limit_bytes=60 * 1024 * 1024
        ),
    )(ci_vectors, alpha_blocks, alpha_cols, beta_blocks, beta_cols, diagonal)


def solution(mesh):
    placed = (
        P(None, "alpha", "beta"),
        P("alpha", None, None, None),
        P("alpha", None),
        P("beta", None, None, None),
        P("beta", None),
        P("alpha", "beta"),
    )
    return jax.shard_map(
        shards, mesh=mesh, in_specs=placed, out_specs=P(None, "alpha", "beta"), check_vma=False
    )
```
